512 devices in a mesh: ctx: 32 (over y, z_hi), head: 16 (over z_lo, x, core).
Axes of the slice: x: 4, y: 8, z: 8 (z_hi: 4, z_lo: 2; z = z_hi * 2 + z_lo), core: 2. Of those that a mesh axis runs over, the one named last changes fastest.
Arguments:
- queries: bfloat16 [16, 8192, 1024], P('head', 'ctx'), may hold values from -6 to 6
- keys: bfloat16 [16, 8192, 128], P('head', 'ctx'), may hold values from -6 to 6
- values: bfloat16 [16, 8192, 128], P('head', 'ctx'), may hold values from -6 to 6
- documents: int32 [16, 8192], P('head', 'ctx'), may hold values from 0 to 3, never falling along the last dimension, each value on 1 to 4096 neighbouring positions
Outputs:
- tokens_out: bfloat16 [16, 8192, 1024], P(None, ('ctx', 'head'))
- log_sums: float32 [16, 8, 8192], P('head', None, 'ctx')
The draws below stay inside these ranges and needn't reach their ends.
Inputs may be any that keep to these rules, and one draw needn't show every extreme that they name: `documents`: each row's ids never fall along positions; each document holds at most half of the 8192 positions.
All inputs are finite; a program needn't handle non-finite values.
Results may differ from the reference program's by a relative error of at most 0.0075.
Values may be sent and summed in bfloat16 or wider, within the bound.
No kernel may reach another device: no remote copies, remote signals or barrier semaphores. Data moves between devices by JAX's collectives and lax.ppermute only.
A program may use at most 64 MiB of HBM per device.

```python
import math
import jax
import jax.numpy as jnp
import numpy as np
from jax import lax

HD = 128
G = 8
SPAN = 256
DOCS = 4
UNITS = 16
L = 8192


def draw_queries(key, part):
    own_key = jax.random.fold_in(key, 1)
    array_shape = (UNITS, L, G * HD)
    return jax.random.truncated_normal(own_key, -6.0, 6.0, array_shape, jnp.float32).astype(jnp.bfloat16)


def draw_keys(key, part):
    own_key = jax.random.fold_in(key, 2)
    array_shape = (UNITS, L, HD)
    return jax.random.truncated_normal(own_key, -6.0, 6.0, array_shape, jnp.float32).astype(jnp.bfloat16)


def levels(key, extent, cuts, low, high):
    def one(axis_at, shards_of):
        heights = jax.random.uniform(jax.random.fold_in(jax.random.fold_in(key, 6), axis_at), (shards_of,), jnp.float32, low / len(cuts), high / len(cuts))
        return jnp.repeat(jnp.exp(heights), extent[axis_at] // shards_of).reshape((-1,) + (1,) * (len(extent) - axis_at - 1))

    gain = one(*cuts[0])
    for cut in cuts[1:]:
        gain = gain * one(*cut)
    return gain


def split_up(amount, total, limit, lean):
    weights = [(1 << 20) // math.isqrt(rank ** lean) + 1 for rank in range(2, amount + 1)]
    spare, given = total - limit - (amount - 1), [1] * (amount - 1)
    while spare > 0:
        movable = [i for i in range(amount - 1) if given[i] < limit]
        pool, left = sum([weights[i] for i in movable]), spare
        for i in movable:
            more = min(limit - given[i], max(1, left * weights[i] // pool), spare)
            given[i] = given[i] + more
            spare = spare - more
    return np.array([limit] + given)


def uneven_parts(key, count, total, limit, slope):
    if count == 2:
        one = jax.random.randint(key, (), max(1, total - limit), min(limit, total - 1) + 1)
        return jnp.stack([one, total - one])
    sizes = jnp.asarray(split_up(count, total, limit, slope), jnp.int32)
    twos = (count - 1) // 2
    donor, receiver = sizes[1:1 + 2 * twos:2], sizes[2:2 + 2 * twos:2]
    room = jnp.minimum(donor - 1, limit - receiver)
    moved = jax.random.randint(jax.random.fold_in(key, 1), (twos,), 0, 1 << 20) % (room + 1)
    sizes = sizes.at[1:1 + 2 * twos:2].set(donor - moved).at[2:2 + 2 * twos:2].set(receiver + moved)
    return sizes[jax.random.permutation(jax.random.fold_in(key, 2), count)]


def gaussian(key, shape, spread, bound, pieces=(), kind=jnp.bfloat16):
    loudness = levels(key, shape, pieces, -0.22, 0.18) if pieces else 1.0
    result = jax.random.normal(key, shape, jnp.float32) * spread * loudness
    return jnp.minimum(jnp.maximum(result, -bound), bound).astype(kind)


def setup_inputs(seed: int = 0) -> dict:
    key_list = jax.random.split(jax.random.key(seed), 5)
    return {
        "queries": draw_queries(jax.random.fold_in(key_list[4], 71), 0),
        "keys": draw_keys(jax.random.fold_in(key_list[4], 71), 0),
        "values": gaussian(key_list[2], (UNITS, L, HD), 1.0, 6.0, ((0, 16), (1, 32))),
        "documents": jax.vmap(lambda own: jnp.searchsorted(jnp.cumsum(uneven_parts(own, DOCS, L, L // 2, 2)), jnp.arange(L), side="right"))(jax.random.split(key_list[3], UNITS)).reshape((UNITS, L)).astype(jnp.int32),
    }


def reference(queries, keys, values, documents):
    score_scale = 1.0 / (HD ** 0.5)
    positions = jnp.arange(L, dtype=jnp.int32)

    def one_unit(unit_data):
        unit_q, unit_k, unit_v, unit_doc = unit_data
        key_f = unit_k.astype(jnp.float32)
        value_f = unit_v.astype(jnp.float32)
        blocked_q = unit_q.reshape(L // SPAN, SPAN, G, HD)
        blocked_pos = positions.reshape(L // SPAN, SPAN)
        blocked_doc = unit_doc.reshape(L // SPAN, SPAN)

        def one_block(query_block):
            query_rows, query_pos, query_doc = query_block
            scores = jnp.einsum("qgd,kd->gqk", query_rows.astype(jnp.float32), key_f) * score_scale
            visible = (positions[None, :] <= query_pos[:, None]) & (unit_doc[None, :] == query_doc[:, None])
            scores = jnp.where(visible[None], scores, -jnp.inf)
            row_max = jnp.max(scores, axis=2)
            weights = jnp.where(visible[None], jnp.exp(scores - row_max[:, :, None]), 0.0)
            row_total = jnp.sum(weights, axis=2)
            rounded = lax.optimization_barrier(weights.astype(jnp.bfloat16))
            mixed_rows = jnp.einsum("gqk,kd->qgd", rounded.astype(jnp.float32), value_f)
            normed = (mixed_rows / jnp.transpose(row_total)[:, :, None]).astype(jnp.bfloat16)
            return normed.reshape(SPAN, G * HD), row_max + jnp.log(row_total)

        unit_outs, unit_lse = lax.map(one_block, (blocked_q, blocked_pos, blocked_doc))
        return unit_outs.reshape(L, G * HD), jnp.transpose(unit_lse, (1, 0, 2)).reshape(G, L)

    tokens_out, log_sums = lax.map(one_unit, (queries, keys, values, documents))
    return tokens_out, log_sums
```

```python
import functools

import jax
import jax.numpy as jnp
import numpy as np
from jax import lax
from jax.experimental import pallas as pl
from jax.experimental.pallas import tpu as pltpu
from jax.sharding import PartitionSpec as P

NEG_FILL = -1e30
ROWS = 4
EXTRA = 8


def attention_kernel(
    scale, shard, groups, head_dim, q_ref, doc_ref, own_ref, row_hbm, near1_hbm, near2_hbm, far_hbm,
    out_ref, lse_ref, buf, key_docs, flags, run_max, run_acc, sems,
):
    place = lax.axis_index("ctx")
    row = place // ROWS
    col = lax.rem(place, ROWS)
    factor = scale * np.log2(np.e)
    sources = (row_hbm, near1_hbm, near2_hbm, far_hbm)
    copies = []
    first = 0
    for index, source in enumerate(sources):
        count = source.shape[0]
        copies.append(
            pltpu.make_async_copy(source, buf.at[pl.ds(first, count)], sems.at[index])
        )
        first += count
    for copy in copies:
        copy.start()

    doc_row = doc_ref[...].astype(jnp.float32)
    query_docs = jnp.transpose(jnp.broadcast_to(doc_row, (128, shard)))
    first_doc = jnp.min(doc_row)
    last_doc = jnp.max(doc_row)

    def attend(keys, vals, lines, fresh):
        vals = jnp.concatenate([vals, jnp.ones_like(vals)], axis=1)
        tiles = keys.shape[0] // 128
        for g in range(groups):
            scores = lax.dot_general(
                q_ref[:, g * head_dim : (g + 1) * head_dim],
                keys,
                (((1,), (1,)), ((), ())),
                preferred_element_type=jnp.float32,
            )
            if lines:
                parts = []
                for j in range(tiles):
                    at = j * 128 % shard
                    keep = query_docs == lines[j * 128 // shard][:, at : at + 128]
                    if fresh:
                        key_at = lax.broadcasted_iota(jnp.int32, (shard, 128), 1) + j * 128
                        keep = keep & (key_at <= lax.broadcasted_iota(jnp.int32, (shard, 128), 0))
                    parts.append(jnp.where(keep, scores[:, j * 128 : (j + 1) * 128], NEG_FILL))
                scores = jnp.concatenate(parts, axis=1)
            top = jnp.max(scores, axis=1, keepdims=True)
            if fresh:
                new_max = jnp.broadcast_to(top, (shard, 128))
            else:
                old_max = run_max[g]
                new_max = jnp.maximum(old_max, top)
            parts = [
                jnp.exp2((scores[:, j * 128 : (j + 1) * 128] - new_max) * factor).astype(jnp.bfloat16)
                for j in range(tiles)
            ]
            weights = jnp.concatenate(parts, axis=1)
            mixed = jnp.dot(weights, vals, preferred_element_type=jnp.float32)
            if fresh:
                run_acc[g] = mixed
            else:
                fade = jnp.exp2((old_max - new_max) * factor)
                run_acc[g, :, :head_dim] = run_acc[g, :, :head_dim] * fade + mixed[:, :head_dim]
                run_acc[g, :, head_dim:] = run_acc[g, :, head_dim:] * fade + mixed[:, head_dim:]
            run_max[g] = new_max

    def attend_pair(pair, masked):
        slots = (2 * pair, 2 * pair + 1)
        keys = jnp.concatenate([buf[slot, :shard, :head_dim] for slot in slots], axis=0)
        vals = jnp.concatenate([buf[slot, :shard, head_dim:] for slot in slots], axis=0)
        attend(keys, vals, [key_docs[slot, 0:1, :] for slot in slots] if masked else [], False)

    attend(own_ref[0, :shard, :head_dim], own_ref[0, :shard, head_dim:], [doc_row], True)

    back = [0] * ROWS + [1] * ROWS + [2] * ROWS + [3, 4] * ROWS
    pairs = len(back) // 2
    for copy in copies:
        copy.wait()
    lines = []
    for slot, rows_back in enumerate(back):
        line = buf[slot, shard : shard + EXTRA, :].astype(jnp.float32)[0:1, :]
        line = jnp.where(row >= rows_back if rows_back else slot < col, line, -1.0)
        key_docs[slot] = jnp.broadcast_to(line, (8, shard))
        lines.append(line)
    for pair in range(pairs):
        low = jnp.min(jnp.minimum(lines[2 * pair], lines[2 * pair + 1]))
        high = jnp.max(jnp.maximum(lines[2 * pair], lines[2 * pair + 1]))
        flags[pair] = jnp.where(high >= first_doc, jnp.where(low == last_doc, 1, 2), 0)

    @pl.loop(0, pairs)
    def _(pair):
        flag = flags[pair]

        @pl.when(flag == 1)
        def _():
            attend_pair(pair, False)

        @pl.when(flag == 2)
        def _():
            attend_pair(pair, True)

    lane = lax.broadcasted_iota(jnp.int32, (shard, 128), 1)
    sums = jnp.zeros((shard, 128), jnp.float32)
    for g in range(groups):
        total = run_acc[g, :, head_dim:]
        out_ref[:, g * head_dim : (g + 1) * head_dim] = (
            run_acc[g, :, :head_dim] / total
        ).astype(jnp.bfloat16)
        sums = jnp.where(lane == g, run_max[g] * scale + jnp.log(total), sums)
    lse_ref[...] = jnp.transpose(sums)[:groups, :]


def attend_rows(queries, docs, own, row, near1, near2, far, head_dim):
    shard, width = queries.shape
    groups = width // head_dim
    slots = row.shape[0] + near1.shape[0] + near2.shape[0] + far.shape[0]
    anywhere = pl.BlockSpec(memory_space=pl.ANY)
    vmem = pl.BlockSpec(memory_space=pltpu.VMEM)
    work = shard * width * slots * shard
    return pl.pallas_call(
        functools.partial(attention_kernel, 1.0 / head_dim**0.5, shard, groups, head_dim),
        out_shape=(
            jax.ShapeDtypeStruct((shard, width), jnp.bfloat16),
            jax.ShapeDtypeStruct((groups, shard), jnp.float32),
        ),
        in_specs=[vmem, vmem, vmem] + [anywhere] * 4,
        out_specs=(vmem, vmem),
        scratch_shapes=[
            pltpu.VMEM((slots, shard + EXTRA, 2 * head_dim), jnp.bfloat16),
            pltpu.VMEM((slots, 8, shard), jnp.float32),
            pltpu.SMEM((16,), jnp.int32),
            pltpu.VMEM((groups, shard, 128), jnp.float32),
            pltpu.VMEM((groups, shard, 2 * head_dim), jnp.float32),
            pltpu.SemaphoreType.DMA((4,)),
        ],
        compiler_params=pltpu.CompilerParams(vmem_limit_bytes=40 << 20),
        cost_estimate=pl.CostEstimate(
            flops=4 * work, bytes_accessed=4 << 20, transcendentals=work // head_dim
        ),
        name="attention",
    )(queries, docs, own, row, near1, near2, far)


def shift(array, rows_on, grid_rows):
    count = grid_rows * ROWS
    pairs = [(place, (place + rows_on * ROWS) % count) for place in range(count)]
    return lax.ppermute(array, "ctx", pairs)


def row_gather(array, grid_rows):
    groups = [[r * ROWS + c for c in range(ROWS)] for r in range(grid_rows)]
    sent = jnp.broadcast_to(array[None], (ROWS, *array.shape))
    got = lax.all_to_all(sent, "ctx", split_axis=0, concat_axis=0, tiled=True, axis_index_groups=groups)
    return got.reshape(ROWS * array.shape[0], *array.shape[1:])


def body(grid_rows, queries, keys, values, documents):
    head_dim = keys.shape[2]
    packed = jnp.concatenate([keys[0], values[0]], axis=1)
    doc_rows = jnp.pad(documents.astype(jnp.bfloat16), ((0, EXTRA - 1), (0, 0)))
    packed = jnp.concatenate([packed, doc_rows], axis=0)[None]
    far3 = shift(packed, 3, grid_rows)
    far4 = shift(packed, 4, grid_rows)
    row = row_gather(packed, grid_rows)
    near1 = shift(row, 1, grid_rows)
    near2 = shift(near1, 1, grid_rows)
    far = row_gather(jnp.concatenate([far3, far4], axis=0), grid_rows)
    out, lse = attend_rows(queries[0], documents, packed, row, near1, near2, far, head_dim)
    parts = lax.axis_size("head")
    blocks = out.reshape(parts, out.shape[0] // parts, out.shape[1])
    tokens = lax.all_to_all(blocks, "head", split_axis=0, concat_axis=0, tiled=True)
    return (tokens, lse[None])


def solution(mesh):
    in_specs = (
        P("head", "ctx", None),
        P("head", "ctx", None),
        P("head", "ctx", None),
        P("head", "ctx"),
    )
    out_specs = (P(None, ("ctx", "head"), None), P("head", None, "ctx"))
    grid_rows = mesh.shape["ctx"] // ROWS
    return jax.shard_map(
        functools.partial(body, grid_rows),
        mesh=mesh,
        in_specs=in_specs,
        out_specs=out_specs,
        check_vma=False,
    )
```

```python
import functools

import jax
import jax.numpy as jnp
import numpy as np
from jax import lax
from jax.experimental import pallas as pl
from jax.experimental.pallas import tpu as pltpu
from jax.sharding import PartitionSpec as P

NEG_FILL = -1e30
ROWS = 4
EXTRA = 8
SPAN = 4


def attention_kernel(sides, backs, has_own, has_state, last, scale, groups, head_dim, *refs):
    refs = list(refs)
    q_ref, doc_ref = refs.pop(0), refs.pop(0)
    own_ref = refs.pop(0) if has_own else None
    sources = [refs.pop(0) for _ in range(max(at for at, _ in sides) + 1)]
    in_state = [refs.pop(0), refs.pop(0)] if has_state else None
    if last:
        out_ref, lse_ref = refs.pop(0), refs.pop(0)
    else:
        out_state = [refs.pop(0), refs.pop(0)]
    buf, key_docs, flags = refs.pop(0), refs.pop(0), refs.pop(0)
    run_max, run_acc = (refs.pop(0), refs.pop(0)) if last else out_state
    sems = refs.pop(0)

    shard = q_ref.shape[0]
    place = lax.axis_index("ctx")
    row = place // ROWS
    col = lax.rem(place, ROWS)
    factor = scale
    copies = []
    for index, (at, side) in enumerate(sides):
        source = sources[at] if side is None else sources[at].at[:, side]
        copies.append(
            pltpu.make_async_copy(source, buf.at[pl.ds(index * ROWS, ROWS)], sems.at[index])
        )
    if has_state:
        copies.append(pltpu.make_async_copy(in_state[0], run_max, sems.at[len(sides)]))
        copies.append(pltpu.make_async_copy(in_state[1], run_acc, sems.at[len(sides) + 1]))
    for copy in copies:
        copy.start()

    doc_row = doc_ref[...].astype(jnp.float32)
    query_docs = jnp.transpose(jnp.broadcast_to(doc_row, (128, shard)))
    first_doc = jnp.min(doc_row)
    last_doc = jnp.max(doc_row)

    def attend(keys, vals, lines, fresh, old):
        vals = jnp.concatenate([vals, jnp.ones_like(vals)], axis=1)
        tiles = keys.shape[0] // 128

        def score(g):
            return lax.dot_general(
                q_ref[:, g * head_dim : (g + 1) * head_dim],
                keys,
                (((1,), (1,)), ((), ())),
                preferred_element_type=jnp.float32,
            )

        ahead = score(0)
        for g in range(groups):
            scores = ahead
            if g + 1 < groups:
                ahead = score(g + 1)
            if lines:
                parts = []
                for j in range(tiles):
                    at = j * 128 % shard
                    keep = query_docs == lines[j * 128 // shard][:, at : at + 128]
                    if fresh:
                        key_at = lax.broadcasted_iota(jnp.int32, (shard, 128), 1) + j * 128
                        keep = keep & (key_at <= lax.broadcasted_iota(jnp.int32, (shard, 128), 0))
                    parts.append(jnp.where(keep, scores[:, j * 128 : (j + 1) * 128], NEG_FILL))
                scores = jnp.concatenate(parts, axis=1)
            top = jnp.max(scores, axis=1, keepdims=True)
            if fresh:
                new_max = jnp.broadcast_to(top, (shard, 128))
            else:
                old_max = old[0][g]
                new_max = jnp.maximum(old_max, top)
            parts = [
                jnp.exp((scores[:, j * 128 : (j + 1) * 128] - new_max) * factor).astype(jnp.bfloat16)
                for j in range(tiles)
            ]
            mixed = jnp.dot(
                jnp.concatenate(parts, axis=1), vals, preferred_element_type=jnp.float32
            )
            if fresh:
                run_acc[g] = mixed
            else:
                fade = jnp.exp((old_max - new_max) * factor)
                run_acc[g, :, :head_dim] = old[1][g, :, :head_dim] * fade + mixed[:, :head_dim]
                run_acc[g, :, head_dim:] = old[1][g, :, head_dim:] * fade + mixed[:, head_dim:]
            run_max[g] = new_max

    def attend_chunk(chunk, masked):
        slots = [SPAN * chunk + j for j in range(SPAN)]
        keys = jnp.concatenate([buf[slot, :shard, :head_dim] for slot in slots], axis=0)
        vals = jnp.concatenate([buf[slot, :shard, head_dim:] for slot in slots], axis=0)
        lines = [key_docs[slot, 0:1, :] for slot in slots] if masked else []
        attend(keys, vals, lines, False, (run_max, run_acc))

    if has_own:
        attend(own_ref[0, :shard, :head_dim], own_ref[0, :shard, head_dim:], [doc_row], True, None)

    chunks = len(backs) * ROWS // SPAN
    for copy in copies:
        copy.wait()
    lines = []
    for index, rows_back in enumerate(backs):
        for at in range(ROWS):
            slot = index * ROWS + at
            line = buf[slot, shard : shard + EXTRA, :].astype(jnp.float32)[0:1, :]
            line = jnp.where(row >= rows_back if rows_back else at < col, line, -1.0)
            key_docs[slot] = jnp.broadcast_to(line, (8, shard))
            lines.append(line)
    for chunk in range(chunks):
        own_lines = lines[SPAN * chunk : SPAN * chunk + SPAN]
        low = jnp.min(functools.reduce(jnp.minimum, own_lines))
        high = jnp.max(functools.reduce(jnp.maximum, own_lines))
        flags[chunk] = jnp.where(high >= first_doc, jnp.where(low == last_doc, 1, 2), 0)

    @pl.loop(0, chunks)
    def _(chunk):
        flag = flags[chunk]

        @pl.when(flag == 1)
        def _():
            attend_chunk(chunk, False)

        @pl.when(flag == 2)
        def _():
            attend_chunk(chunk, True)

    if last:
        lane = lax.broadcasted_iota(jnp.int32, (shard, 128), 1)
        sums = jnp.zeros((shard, 128), jnp.float32)
        for g in range(groups):
            total = run_acc[g, :, head_dim:]
            out_ref[:, g * head_dim : (g + 1) * head_dim] = (
                run_acc[g, :, :head_dim] / total
            ).astype(jnp.bfloat16)
            sums = jnp.where(lane == g, run_max[g] * scale + jnp.log(total), sums)
        lse_ref[...] = jnp.transpose(sums)[:groups, :]


def attend_rows(queries, docs, own, state, arrays, sides, backs, last, weight=1):
    shard, width = queries.shape
    head_dim = arrays[0].shape[-1] // 2
    groups = width // head_dim
    anywhere = pl.BlockSpec(memory_space=pl.ANY)
    vmem = pl.BlockSpec(memory_space=pltpu.VMEM)
    state_shapes = [
        jax.ShapeDtypeStruct((groups, shard, 128), jnp.float32),
        jax.ShapeDtypeStruct((groups, shard, 2 * head_dim), jnp.float32),
    ]
    result = [
        jax.ShapeDtypeStruct((shard, width), jnp.bfloat16),
        jax.ShapeDtypeStruct((groups, shard), jnp.float32),
    ]
    slots = ROWS * len(sides)
    args = [queries, docs] + ([own] if own is not None else []) + list(arrays) + list(state or [])
    starts = len(args) - len(arrays) - len(state or [])
    specs = [vmem] * starts + [anywhere] * (len(args) - starts)
    scratch = [
        pltpu.VMEM((slots, shard + EXTRA, 2 * head_dim), jnp.bfloat16),
        pltpu.VMEM((slots, 8, shard), jnp.float32),
        pltpu.SMEM((slots // SPAN,), jnp.int32),
    ]
    if last:
        scratch += [pltpu.VMEM(s.shape, s.dtype) for s in state_shapes]
    scratch.append(pltpu.SemaphoreType.DMA((len(sides) + 2,)))
    work = shard * width * (slots + (own is not None)) * shard
    return pl.pallas_call(
        functools.partial(
            attention_kernel, tuple(sides), tuple(backs), own is not None, state is not None, last,
            1.0 / head_dim**0.5, groups, head_dim,
        ),
        out_shape=tuple(result if last else state_shapes),
        in_specs=specs,
        out_specs=(vmem, vmem),
        scratch_shapes=scratch,
        compiler_params=pltpu.CompilerParams(vmem_limit_bytes=16 << 20),
        cost_estimate=pl.CostEstimate(
            flops=4 * work * weight, bytes_accessed=4 << 20, transcendentals=work // head_dim
        ),
        name="attention",
    )(*args)

def shift(array, rows_on, grid_rows):
    count = grid_rows * ROWS
    pairs = [(place, (place + rows_on * ROWS) % count) for place in range(count)]
    return lax.ppermute(array, "ctx", pairs)


def row_gather(array, grid_rows):
    groups = [[r * ROWS + c for c in range(ROWS)] for r in range(grid_rows)]
    sent = jnp.broadcast_to(array[None], (ROWS, *array.shape))
    return lax.all_to_all(sent, "ctx", split_axis=0, concat_axis=0, tiled=True, axis_index_groups=groups)


def spread_kernel(first_ref, second_ref, after_ref, out_ref):
    for at in range(ROWS):
        out_ref[at, 0] = first_ref[...]
        out_ref[at, 1] = second_ref[...]


def spread(first, second, after):
    vmem = pl.BlockSpec(memory_space=pltpu.VMEM)
    return pl.pallas_call(
        spread_kernel,
        out_shape=jax.ShapeDtypeStruct((ROWS, 2, *first.shape), first.dtype),
        in_specs=[vmem, vmem, pl.BlockSpec(memory_space=pl.ANY)],
        out_specs=vmem,
        cost_estimate=pl.CostEstimate(flops=100 * 10**9, bytes_accessed=4 << 20, transcendentals=0),
        name="spread",
    )(first, second, after)


def exchange(sent, grid_rows):
    groups = [[r * ROWS + c for c in range(ROWS)] for r in range(grid_rows)]
    return lax.all_to_all(sent, "ctx", split_axis=0, concat_axis=0, tiled=True, axis_index_groups=groups)


def pack(keys, values, documents):
    packed = jnp.concatenate([keys[0], values[0]], axis=1)
    doc_rows = jnp.pad(documents.astype(jnp.bfloat16), ((0, EXTRA - 1), (0, 0)))
    return jnp.concatenate([packed, doc_rows], axis=0)


def body(grid_rows, queries, keys, values, documents):
    packed = pack(keys, values, documents)
    row = row_gather(packed, grid_rows)
    far3 = shift(packed, 3, grid_rows)
    far4 = shift(packed, 4, grid_rows)
    near1 = shift(row, 1, grid_rows)
    state = attend_rows(queries[0], documents, packed[None], None, [row], [(0, None)], [0], False, 1)
    far = exchange(spread(far3, far4, row), grid_rows)
    near1, state = lax.optimization_barrier((near1, state))
    near2 = shift(near1, 1, grid_rows)
    state = attend_rows(queries[0], documents, None, state, [near1], [(0, None)], [1], False, 1000)
    state = attend_rows(queries[0], documents, None, state, [near2], [(0, None)], [2], False)
    out, lse = attend_rows(queries[0], documents, None, state, [far], [(0, 0), (0, 1)], [3, 4], True)
    parts = lax.axis_size("head")
    blocks = out.reshape(parts, out.shape[0] // parts, out.shape[1])
    tokens = lax.all_to_all(blocks, "head", split_axis=0, concat_axis=0, tiled=True)
    return (tokens, lse[None])


def solution(mesh):
    in_specs = (
        P("head", "ctx", None),
        P("head", "ctx", None),
        P("head", "ctx", None),
        P("head", "ctx"),
    )
    out_specs = (P(None, ("ctx", "head"), None), P("head", None, "ctx"))
    grid_rows = mesh.shape["ctx"] // ROWS
    return jax.shard_map(
        functools.partial(body, grid_rows),
        mesh=mesh,
        in_specs=in_specs,
        out_specs=out_specs,
        check_vma=False,
    )
```

```python
import functools

import jax
import jax.numpy as jnp
import numpy as np
from jax import lax
from jax.experimental import pallas as pl
from jax.experimental.pallas import tpu as pltpu
from jax.sharding import PartitionSpec as P

NEG_FILL = -1e30
ROWS = 4
EXTRA = 8
SPAN = 4


def attention_kernel(sides, backs, has_own, has_state, last, scale, groups, head_dim, *refs):
    refs = list(refs)
    q_ref, doc_ref = refs.pop(0), refs.pop(0)
    own_ref = refs.pop(0) if has_own else None
    sources = [refs.pop(0) for _ in range(max(at for at, _ in sides) + 1)]
    in_state = [refs.pop(0), refs.pop(0)] if has_state else None
    if last:
        out_ref, lse_ref = refs.pop(0), refs.pop(0)
    else:
        out_state = [refs.pop(0), refs.pop(0)]
    buf, key_docs, flags = refs.pop(0), refs.pop(0), refs.pop(0)
    run_max, run_acc = (refs.pop(0), refs.pop(0)) if last else out_state
    sems = refs.pop(0)

    shard = q_ref.shape[0]
    place = lax.axis_index("ctx")
    row = place // ROWS
    col = lax.rem(place, ROWS)
    factor = scale
    copies = []
    for index, (at, side) in enumerate(sides):
        source = sources[at] if side is None else sources[at].at[:, side]
        copies.append(
            pltpu.make_async_copy(source, buf.at[pl.ds(index * ROWS, ROWS)], sems.at[index])
        )
    if has_state:
        copies.append(pltpu.make_async_copy(in_state[0], run_max, sems.at[len(sides)]))
        copies.append(pltpu.make_async_copy(in_state[1], run_acc, sems.at[len(sides) + 1]))
    for copy in copies:
        copy.start()

    doc_row = doc_ref[...].astype(jnp.float32)
    query_docs = jnp.transpose(jnp.broadcast_to(doc_row, (128, shard)))
    first_doc = jnp.min(doc_row)
    last_doc = jnp.max(doc_row)

    def attend(keys, vals, lines, fresh, old):
        vals = jnp.concatenate([vals, jnp.ones_like(vals)], axis=1)
        tiles = keys.shape[0] // 128

        def score(g):
            return lax.dot_general(
                q_ref[:, g * head_dim : (g + 1) * head_dim],
                keys,
                (((1,), (1,)), ((), ())),
                preferred_element_type=jnp.float32,
            )

        ahead = score(0)
        for g in range(groups):
            scores = ahead
            if g + 1 < groups:
                ahead = score(g + 1)
            if lines:
                parts = []
                for j in range(tiles):
                    at = j * 128 % shard
                    keep = query_docs == lines[j * 128 // shard][:, at : at + 128]
                    if fresh:
                        key_at = lax.broadcasted_iota(jnp.int32, (shard, 128), 1) + j * 128
                        keep = keep & (key_at <= lax.broadcasted_iota(jnp.int32, (shard, 128), 0))
                    parts.append(jnp.where(keep, scores[:, j * 128 : (j + 1) * 128], NEG_FILL))
                scores = jnp.concatenate(parts, axis=1)
            top = jnp.max(scores, axis=1, keepdims=True)
            if fresh:
                new_max = jnp.broadcast_to(top, (shard, 128))
            else:
                old_max = old[0][g]
                new_max = jnp.maximum(old_max, top)
            parts = [
                jnp.exp((scores[:, j * 128 : (j + 1) * 128] - new_max) * factor).astype(jnp.bfloat16)
                for j in range(tiles)
            ]
            mixed = jnp.dot(
                jnp.concatenate(parts, axis=1), vals, preferred_element_type=jnp.float32
            )
            if fresh:
                run_acc[g] = mixed
            else:
                fade = jnp.exp((old_max - new_max) * factor)
                run_acc[g, :, :head_dim] = old[1][g, :, :head_dim] * fade + mixed[:, :head_dim]
                run_acc[g, :, head_dim:] = old[1][g, :, head_dim:] * fade + mixed[:, head_dim:]
            run_max[g] = new_max

    def attend_chunk(chunk, masked):
        slots = [SPAN * chunk + j for j in range(SPAN)]
        keys = jnp.concatenate([buf[slot, :shard, :head_dim] for slot in slots], axis=0)
        vals = jnp.concatenate([buf[slot, :shard, head_dim:] for slot in slots], axis=0)
        lines = [key_docs[slot, 0:1, :] for slot in slots] if masked else []
        attend(keys, vals, lines, False, (run_max, run_acc))

    if has_own:
        attend(own_ref[0, :shard, :head_dim], own_ref[0, :shard, head_dim:], [doc_row], True, None)

    chunks = len(backs) * ROWS // SPAN
    for copy in copies:
        copy.wait()
    lines = []
    for index, rows_back in enumerate(backs):
        for at in range(ROWS):
            slot = index * ROWS + at
            line = buf[slot, shard : shard + EXTRA, :].astype(jnp.float32)[0:1, :]
            line = jnp.where(row >= rows_back if rows_back else at < col, line, -1.0)
            key_docs[slot] = jnp.broadcast_to(line, (8, shard))
            lines.append(line)
    for chunk in range(chunks):
        own_lines = lines[SPAN * chunk : SPAN * chunk + SPAN]
        low = jnp.min(functools.reduce(jnp.minimum, own_lines))
        high = jnp.max(functools.reduce(jnp.maximum, own_lines))
        flags[chunk] = jnp.where(high >= first_doc, jnp.where(low == last_doc, 1, 2), 0)

    @pl.loop(0, chunks)
    def _(chunk):
        flag = flags[chunk]

        @pl.when(flag == 1)
        def _():
            attend_chunk(chunk, False)

        @pl.when(flag == 2)
        def _():
            attend_chunk(chunk, True)

    if last:
        lane = lax.broadcasted_iota(jnp.int32, (shard, 128), 1)
        sums = jnp.zeros((shard, 128), jnp.float32)
        for g in range(groups):
            total = run_acc[g, :, head_dim:]
            out_ref[:, g * head_dim : (g + 1) * head_dim] = (
                run_acc[g, :, :head_dim] / total
            ).astype(jnp.bfloat16)
            sums = jnp.where(lane == g, run_max[g] * scale + jnp.log(total), sums)
        lse_ref[...] = jnp.transpose(sums)[:groups, :]


def attend_rows(queries, docs, own, state, arrays, sides, backs, last, weight=1):
    shard, width = queries.shape
    head_dim = arrays[0].shape[-1] // 2
    groups = width // head_dim
    anywhere = pl.BlockSpec(memory_space=pl.ANY)
    vmem = pl.BlockSpec(memory_space=pltpu.VMEM)
    state_shapes = [
        jax.ShapeDtypeStruct((groups, shard, 128), jnp.float32),
        jax.ShapeDtypeStruct((groups, shard, 2 * head_dim), jnp.float32),
    ]
    result = [
        jax.ShapeDtypeStruct((shard, width), jnp.bfloat16),
        jax.ShapeDtypeStruct((groups, shard), jnp.float32),
    ]
    slots = ROWS * len(sides)
    args = [queries, docs] + ([own] if own is not None else []) + list(arrays) + list(state or [])
    starts = len(args) - len(arrays) - len(state or [])
    specs = [vmem] * starts + [anywhere] * (len(args) - starts)
    scratch = [
        pltpu.VMEM((slots, shard + EXTRA, 2 * head_dim), jnp.bfloat16),
        pltpu.VMEM((slots, 8, shard), jnp.float32),
        pltpu.SMEM((slots // SPAN,), jnp.int32),
    ]
    if last:
        scratch += [pltpu.VMEM(s.shape, s.dtype) for s in state_shapes]
    scratch.append(pltpu.SemaphoreType.DMA((len(sides) + 2,)))
    work = shard * width * (slots + (own is not None)) * shard
    return pl.pallas_call(
        functools.partial(
            attention_kernel, tuple(sides), tuple(backs), own is not None, state is not None, last,
            1.0 / head_dim**0.5, groups, head_dim,
        ),
        out_shape=tuple(result if last else state_shapes),
        in_specs=specs,
        out_specs=(vmem, vmem),
        scratch_shapes=scratch,
        compiler_params=pltpu.CompilerParams(vmem_limit_bytes=16 << 20),
        cost_estimate=pl.CostEstimate(
            flops=4 * work * weight, bytes_accessed=4 << 20, transcendentals=work // head_dim
        ),
        name="attention",
    )(*args)

def shift(array, rows_on, grid_rows):
    count = grid_rows * ROWS
    pairs = [(place, (place + rows_on * ROWS) % count) for place in range(count)]
    return lax.ppermute(array, "ctx", pairs)


def spread_kernel(first_ref, second_ref, after_ref, out_ref):
    for at in range(ROWS):
        out_ref[at, 0] = first_ref[...]
        out_ref[at, 1] = second_ref[...]


def spread(first, second, after):
    vmem = pl.BlockSpec(memory_space=pltpu.VMEM)
    return pl.pallas_call(
        spread_kernel,
        out_shape=jax.ShapeDtypeStruct((ROWS, 2, *first.shape), first.dtype),
        in_specs=[vmem, vmem, pl.BlockSpec(memory_space=pl.ANY)],
        out_specs=vmem,
        cost_estimate=pl.CostEstimate(flops=100 * 10**9, bytes_accessed=4 << 20, transcendentals=0),
        name="spread",
    )(first, second, after)


def exchange(sent, grid_rows):
    groups = [[r * ROWS + c for c in range(ROWS)] for r in range(grid_rows)]
    return lax.all_to_all(sent, "ctx", split_axis=0, concat_axis=0, tiled=True, axis_index_groups=groups)


def pack_kernel(key_ref, value_ref, doc_ref, packed_ref, sent_ref):
    shard, head_dim = key_ref.shape
    docs = doc_ref[...].astype(jnp.float32)
    first = lax.broadcasted_iota(jnp.int32, (EXTRA, shard), 0) == 0
    docs = jnp.where(first, docs, 0.0).astype(jnp.bfloat16)
    for ref in [packed_ref.at[0]] + [sent_ref.at[at] for at in range(ROWS)]:
        ref[:shard, :head_dim] = key_ref[...]
        ref[:shard, head_dim:] = value_ref[...]
        ref[shard:, :] = docs


def pack(keys, values, documents):
    shard, head_dim = keys.shape
    block = (shard + EXTRA, 2 * head_dim)
    vmem = pl.BlockSpec(memory_space=pltpu.VMEM)
    return pl.pallas_call(
        pack_kernel,
        out_shape=(
            jax.ShapeDtypeStruct((1, *block), keys.dtype),
            jax.ShapeDtypeStruct((ROWS, *block), keys.dtype),
        ),
        in_specs=[vmem] * 3,
        out_specs=(vmem, vmem),
        name="pack",
    )(keys, values, documents)


def body(grid_rows, queries, keys, values, documents):
    packed, sent = pack(keys[0], values[0], documents)
    row = exchange(sent, grid_rows)
    far3 = shift(packed, 3, grid_rows)
    far4 = shift(packed, 4, grid_rows)
    near1 = shift(row, 1, grid_rows)
    state = attend_rows(queries[0], documents, packed, None, [row], [(0, None)], [0], False, 1)
    far = exchange(spread(far3[0], far4[0], row), grid_rows)
    near2 = shift(near1, 1, grid_rows)
    state = attend_rows(queries[0], documents, None, state, [near1], [(0, None)], [1], False, 1000)
    state = attend_rows(queries[0], documents, None, state, [near2], [(0, None)], [2], False)
    out, lse = attend_rows(queries[0], documents, None, state, [far], [(0, 0), (0, 1)], [3, 4], True)
    parts = lax.axis_size("head")
    blocks = out.reshape(parts, out.shape[0] // parts, out.shape[1])
    tokens = lax.all_to_all(blocks, "head", split_axis=0, concat_axis=0, tiled=True)
    return (tokens, lse[None])


def solution(mesh):
    in_specs = (
        P("head", "ctx", None),
        P("head", "ctx", None),
        P("head", "ctx", None),
        P("head", "ctx"),
    )
    out_specs = (P(None, ("ctx", "head"), None), P("head", None, "ctx"))
    grid_rows = mesh.shape["ctx"] // ROWS
    return jax.shard_map(
        functools.partial(body, grid_rows),
        mesh=mesh,
        in_specs=in_specs,
        out_specs=out_specs,
        check_vma=False,
    )
```
